512 devices in a mesh: section: 16 (over y, core), ctx: 32 (over x, z).
Axes of the slice: x: 4, y: 8, z: 8, core: 2. Of those that a mesh axis runs over, the one named last changes fastest.
Arguments:
- query_rows: bfloat16 [65536, 4096], P(('section', 'ctx')), may hold values from -6 to 6
- key_rows: bfloat16 [65536, 4096], P(('section', 'ctx')), may hold values from -6 to 6
- value_rows: bfloat16 [65536, 4096], P(('section', 'ctx')), may hold values from -6 to 6
- short_taps: bfloat16 [16, 3, 3, 4096], P('section', None, None, 'ctx'), may hold values from -3 to 3
- long_taps: bfloat16 [16, 4096, 128], P('section', 'ctx'), may hold values from -0.5 to 0.5
- skip_gain: bfloat16 [16, 4096], P('section', 'ctx'), may hold values from 0.5 to 1.5
- prior_qkv: bfloat16 [16, 3, 2, 4096], P('section', None, None, 'ctx'), may hold values from -6 to 6
- prior_product: bfloat16 [16, 127, 4096], P('section', None, 'ctx'), may hold values from -6 to 6
Outputs:
- handed: bfloat16 [65536, 4096], P(('section', 'ctx'))
The draws below stay inside these ranges and needn't reach their ends.
All inputs are finite; a program needn't handle non-finite values.
Results may differ from the reference program's by a relative error of at most 0.005.
Values may be sent and summed in bfloat16 or wider, within the bound.
No kernel may reach another device: no remote copies, remote signals or barrier semaphores. Data moves between devices by JAX's collectives and lax.ppermute only.
A program may use at most 128 MiB of HBM per device.

```python
import jax
import jax.numpy as jnp
from jax import lax

C = 4096
TAPS = 128
SHORT = 3
LENGTH = 4096
ROWS = 65536
N_SECTION = 16


def block_levels(rng, dims, cuts, low, top_value):
    def one(dim, shards_of):
        draws = jax.random.uniform(jax.random.fold_in(jax.random.fold_in(rng, 6), dim), (shards_of,), jnp.float32, low / len(cuts), top_value / len(cuts))
        return jnp.repeat(jnp.exp(draws), dims[dim] // shards_of).reshape((-1,) + (1,) * (len(dims) - dim - 1))

    factor_of = one(*cuts[0])
    for cut in cuts[1:]:
        factor_of = factor_of * one(*cut)
    return factor_of


def scatter_about(rng, dims, scale, reach, shards=(), kind=jnp.bfloat16):
    result = jax.random.normal(rng, dims, jnp.float32) * scale
    if len(shards) > 0:
        result = block_levels(rng, dims, shards, -0.22, 0.18) * result
    return jnp.clip(result, min=-reach, max=reach).astype(kind)


def setup_inputs(seed: int = 0) -> dict:
    arg_keys = jax.random.split(jax.random.key(seed), 9)
    query_rows = scatter_about(arg_keys[0], (ROWS, C), 1.0, 6.0, ((0, 512),))
    key_rows = scatter_about(arg_keys[1], (ROWS, C), 1.0, 6.0, ((0, 512),))
    value_rows = scatter_about(arg_keys[2], (ROWS, C), 1.0, 6.0, ((0, 512),))
    short_taps = scatter_about(arg_keys[3], (N_SECTION, 3, SHORT, C), 0.6, 3.0, ((0, 16), (3, 32)))
    long_taps = scatter_about(arg_keys[4], (N_SECTION, C, TAPS), 0.088, 0.5, ((0, 16), (1, 32)))
    skip_gain = jnp.clip(1.0 + 0.1 * jax.random.normal(arg_keys[5], (N_SECTION, C), jnp.float32), 0.5, 1.5).astype(jnp.bfloat16)
    prior_qkv = scatter_about(arg_keys[6], (N_SECTION, 3, 2, C), 1.0, 6.0, ((0, 16), (3, 32)))
    prior_product = scatter_about(arg_keys[7], (N_SECTION, 127, C), 1.0, 6.0, ((0, 16), (2, 32)))
    return dict(query_rows=query_rows, key_rows=key_rows, value_rows=value_rows, short_taps=short_taps, long_taps=long_taps, skip_gain=skip_gain, prior_qkv=prior_qkv, prior_product=prior_product)


def featurize(rows, history, taps):
    padded = jnp.concatenate([history, rows], axis=0).astype(jnp.float32)
    weights = taps.astype(jnp.float32)
    return weights[0] * padded[2:] + weights[1] * padded[1:-1] + weights[2] * padded[:-2]


def one_section(pieces):
    query_rows, key_rows, value_rows, short_taps, long_taps, skip_gain, prior_qkv, prior_product = pieces
    query_feat = featurize(query_rows, prior_qkv[0], short_taps[0])
    key_feat = featurize(key_rows, prior_qkv[1], short_taps[1])
    value_feat = featurize(value_rows, prior_qkv[2], short_taps[2])
    product = (key_feat * value_feat).astype(jnp.bfloat16)
    product_f = product.astype(jnp.float32)
    extended = jnp.concatenate([prior_product.astype(jnp.float32), product_f], axis=0)
    spectrum = jnp.fft.rfft(extended, n=2 * LENGTH, axis=0) * jnp.fft.rfft(long_taps.astype(jnp.float32).T, n=2 * LENGTH, axis=0)
    filtered = jnp.fft.irfft(spectrum, n=2 * LENGTH, axis=0)[127:127 + LENGTH].astype(jnp.float32)
    mixed = query_feat * (filtered + skip_gain.astype(jnp.float32) * product_f)
    return mixed.astype(jnp.bfloat16)


def reference(query_rows, key_rows, value_rows, short_taps, long_taps, skip_gain, prior_qkv, prior_product):
    shape = (N_SECTION, LENGTH, C)
    mixed = lax.map(one_section, (query_rows.reshape(shape), key_rows.reshape(shape), value_rows.reshape(shape), short_taps, long_taps, skip_gain, prior_qkv, prior_product))
    handed = jnp.concatenate([mixed[-1:], mixed[:-1]], axis=0)
    return handed.reshape(N_SECTION * LENGTH, C)
```

```python
import jax
import jax.numpy as jnp
import numpy as np
from jax import lax
from jax.experimental import pallas as pl
from jax.experimental.pallas import tpu as pltpu
from jax.sharding import Mesh
from jax.sharding import PartitionSpec as P

BF = jnp.bfloat16
F32 = jnp.float32
CHUNKS = 2
WIDTH = 512


def split_hi_lo(matrix):
    high = matrix.astype(np.float32).astype(BF)
    low = (matrix - high.astype(np.float64)).astype(np.float32).astype(BF)
    return high, low


def dft_matrices():
    n = np.arange(256, dtype=np.float64)[None, :]
    k = np.arange(128, dtype=np.float64)[:, None]
    angle = np.pi * (2 * k + 1) * n / 256
    forward = np.concatenate([np.cos(angle), np.sin(angle)], axis=0)
    inverse = forward.T[128:] / 128
    return split_hi_lo(forward), split_hi_lo(inverse)


def dot(a, b):
    return lax.dot_general(a, b, (((1,), (0,)), ((), ())), preferred_element_type=F32)


def dot_nt(a, b):
    return lax.dot_general(a, b, (((1,), (1,)), ((), ())), preferred_element_type=F32)


def featurize(rows, before, weights):
    index = lax.broadcasted_iota(jnp.int32, rows.shape, 0)
    back_one = jnp.where(index == 0, before[1:2], pltpu.roll(rows, 1, 0))
    back_two = jnp.where(
        index == 0, before[0:1], jnp.where(index == 1, before[1:2], pltpu.roll(rows, 2, 0))
    )
    return weights[0:1] * rows + weights[1:2] * back_one + weights[2:3] * back_two


def edges_of(first, small, edge):
    return jnp.where(first, small[10:16], edge[0:6])


def product_kernel(first_ref, key_ref, value_ref, edge_ref, small_ref, out_ref):
    first = first_ref[0] != 0
    for g in range(WIDTH // 128):
        cols = pl.ds(g * 128, 128)
        small = small_ref[g].astype(F32)
        edge = edges_of(first, small, edge_ref[:, cols].astype(F32))
        key = featurize(key_ref[:, cols].astype(F32), edge[2:4], small[3:6])
        value = featurize(value_ref[:, cols].astype(F32), edge[4:6], small[6:9])
        out_ref[:, cols] = (key * value).astype(BF)


def filter_kernel(
    first_ref,
    query_ref,
    edge_ref,
    small_ref,
    own_ref,
    halo_ref,
    wide_ref,
    fwd_hi_ref,
    fwd_lo_ref,
    inv_hi_ref,
    inv_lo_ref,
    out_ref,
):
    first = first_ref[0] != 0
    for g in range(WIDTH // 128):
        cols = pl.ds(g * 128, 128)
        small = small_ref[g].astype(F32)
        edge = edges_of(first, small, edge_ref[:, cols].astype(F32))
        query = featurize(query_ref[:, cols].astype(F32), edge[0:2], small[0:3])
        own = own_ref[:, cols]
        prior = wide_ref[g, 128:256].astype(F32)
        before = jnp.where(first, prior, halo_ref[:, cols].astype(F32)).astype(BF)
        signal = jnp.concatenate([before, own], axis=0)
        taps = wide_ref[g, 0:128]
        spec_x = dot(fwd_hi_ref[...], signal) + dot(fwd_lo_ref[...], signal)
        spec_h = dot_nt(fwd_hi_ref[:, 0:128], taps) + dot_nt(fwd_lo_ref[:, 0:128], taps)
        xc, xs, hc, hs = spec_x[:128], spec_x[128:], spec_h[:128], spec_h[128:]
        spec_y = jnp.concatenate([xc * hc - xs * hs, xc * hs + xs * hc], axis=0)
        y_hi = spec_y.astype(BF)
        y_lo = (spec_y - y_hi.astype(F32)).astype(BF)
        inv_hi = inv_hi_ref[...]
        filtered = dot(inv_hi, y_hi) + dot(inv_hi, y_lo) + dot(inv_lo_ref[...], y_hi)
        mixed = query * (filtered + small[9:10] * own.astype(F32))
        out_ref[:, cols] = mixed.astype(BF)


def shift_by_one(value, axes, count):
    return lax.ppermute(value, axes, [(i, (i + 1) % count) for i in range(count)])


def spread(value, axis, count):
    copies = jnp.broadcast_to(value[None], (count,) + value.shape)
    return lax.all_to_all(copies, axis, split_axis=0, concat_axis=0, tiled=True)


def whole(shape):
    return pl.BlockSpec(shape, lambda j: (0,) * len(shape))


def body(
    query_rows, key_rows, value_rows, short_taps, long_taps, skip_gain, prior_qkv, prior_product
):
    n_x, n_z = lax.axis_size("ctx_x"), lax.axis_size("ctx_z")
    n_ctx = n_x * n_z
    n_section = lax.axis_size("section")
    rows, channels = query_rows.shape
    ctx = ("ctx_x", "ctx_z")
    first = (lax.axis_index(ctx) == 0).astype(jnp.int32).reshape(1)

    small = jnp.concatenate(
        [short_taps[0].reshape(9, 128), skip_gain, prior_qkv[0].reshape(6, 128)], axis=0
    )
    smalls = spread(small, ctx, n_ctx)
    last = jnp.concatenate(
        [query_rows[-2:], key_rows[-2:], value_rows[-2:], value_rows[-2:]], axis=0
    )
    edge = shift_by_one(last, ctx, n_ctx)
    wide = jnp.concatenate(
        [long_taps[0], jnp.zeros((1, 128), BF), prior_product[0]], axis=0
    )
    wides = spread(spread(wide, "ctx_z", n_z), "ctx_x", n_x).reshape(n_ctx, 256, 128)

    (fwd_hi, fwd_lo), (inv_hi, inv_lo) = dft_matrices()
    span = channels // CHUNKS
    steps = span // WIDTH
    groups = WIDTH // 128
    smem = pl.BlockSpec(memory_space=pltpu.SMEM)
    params = pltpu.CompilerParams(vmem_limit_bytes=48 * 1024 * 1024)

    def at(chunk):
        return lambda j: (0, chunk * steps + j)

    def at_group(chunk):
        return lambda j: (chunk * steps + j, 0, 0)

    products = []
    for chunk in range(CHUNKS):
        products.append(
            pl.pallas_call(
                product_kernel,
                grid=(steps,),
                in_specs=[
                    smem,
                    pl.BlockSpec((rows, WIDTH), at(chunk)),
                    pl.BlockSpec((rows, WIDTH), at(chunk)),
                    pl.BlockSpec((8, WIDTH), at(chunk)),
                    pl.BlockSpec((groups, 16, 128), at_group(chunk)),
                ],
                out_specs=pl.BlockSpec((rows, WIDTH), lambda j: (0, j)),
                out_shape=jax.ShapeDtypeStruct((rows, span), BF),
                compiler_params=params,
                name="gated_product",
            )(first, key_rows, value_rows, edge, smalls)
        )
    halos = [shift_by_one(product, ctx, n_ctx) for product in products]
    handed = []
    for chunk in range(CHUNKS):
        mixed = pl.pallas_call(
            filter_kernel,
            grid=(steps,),
            in_specs=[
                smem,
                pl.BlockSpec((rows, WIDTH), at(chunk)),
                pl.BlockSpec((8, WIDTH), at(chunk)),
                pl.BlockSpec((groups, 16, 128), at_group(chunk)),
                pl.BlockSpec((rows, WIDTH), lambda j: (0, j)),
                pl.BlockSpec((rows, WIDTH), lambda j: (0, j)),
                pl.BlockSpec((groups, 256, 128), at_group(chunk)),
                whole((256, 256)),
                whole((256, 256)),
                whole((128, 256)),
                whole((128, 256)),
            ],
            out_specs=pl.BlockSpec((rows, WIDTH), lambda j: (0, j)),
            out_shape=jax.ShapeDtypeStruct((rows, span), BF),
            compiler_params=params,
            name="filter_and_gate",
        )(
            first, query_rows, edge, smalls, products[chunk], halos[chunk], wides,
            fwd_hi, fwd_lo, inv_hi, inv_lo,
        )
        handed.append(shift_by_one(mixed, "section", n_section))
    return jnp.concatenate(handed, axis=1)


def solution(mesh):
    n_ctx = mesh.shape["ctx"]
    n_z = 8
    inner = Mesh(
        mesh.devices.reshape(mesh.shape["section"], n_ctx // n_z, n_z), ("section", "ctx_x", "ctx_z")
    )
    ctx = ("ctx_x", "ctx_z")
    in_specs = (
        P(("section",) + ctx, None),
        P(("section",) + ctx, None),
        P(("section",) + ctx, None),
        P("section", None, None, ctx),
        P("section", ctx, None),
        P("section", ctx),
        P("section", None, None, ctx),
        P("section", None, ctx),
    )
    out_specs = P(("section",) + ctx, None)
    return jax.shard_map(body, mesh=inner, in_specs=in_specs, out_specs=out_specs, check_vma=False)
```

```python
import functools

import jax
import jax.numpy as jnp
import numpy as np
from jax import lax
from jax.experimental import pallas as pl
from jax.experimental.pallas import tpu as pltpu
from jax.sharding import Mesh
from jax.sharding import PartitionSpec as P

BF = jnp.bfloat16
F32 = jnp.float32
STEP = 512
BLOCKS = ((0, 1), (2, 3))
HINT = 20 * 10**9


def stacked_hi_lo(matrix):
    high = matrix.astype(np.float32).astype(BF)
    low = (matrix - high.astype(np.float64)).astype(np.float32).astype(BF)
    return np.concatenate([high, low], axis=0)


def dft_matrices():
    n = np.arange(256, dtype=np.float64)[None, :]
    k = np.arange(128, dtype=np.float64)[:, None]
    angle = np.pi * (2 * k + 1) * n / 256
    forward = np.concatenate([np.cos(angle), np.sin(angle)], axis=0)
    inverse = forward.T[128:] / 128
    return stacked_hi_lo(forward), stacked_hi_lo(inverse)


def dot(a, b):
    return lax.dot_general(a, b, (((1,), (0,)), ((), ())), preferred_element_type=F32)


def dot_nt(a, b):
    return lax.dot_general(a, b, (((1,), (1,)), ((), ())), preferred_element_type=F32)


def featurize(rows, before, weights):
    index = lax.broadcasted_iota(jnp.int32, rows.shape, 0)
    back_one = jnp.where(index == 0, before[1:2], pltpu.roll(rows, 1, 0))
    back_two = jnp.where(
        index == 0, before[0:1], jnp.where(index == 1, before[1:2], pltpu.roll(rows, 2, 0))
    )
    return weights[0:1] * rows + weights[1:2] * back_one + weights[2:3] * back_two


def edges_of(first, small, edge):
    return jnp.where(first, small[10:16], edge[0:6])


def small_at(ref, start, count):
    parts = []
    for g in range(start, start + count):
        low = 128 + 16 * (g // 8)
        parts.append(ref[g % 8, low : low + 16].astype(F32))
    return jnp.concatenate(parts, axis=1)


def lanes(ref, start, count):
    return jnp.concatenate([ref[start + i].astype(F32) for i in range(count)], axis=1)


def prepare_kernel(
    query_ref, key_ref, value_ref, short_ref, gain_ref, qkv_ref, prior_ref,
    edge_ref, small_ref, tail_ref,
):
    ends = [ref[...].astype(F32)[6:8] for ref in (query_ref, key_ref, value_ref)]
    edge_ref[...] = jnp.concatenate(ends + ends[2:], axis=0).astype(BF)
    parts = [short_ref[0, m].astype(F32) for m in range(3)] + [gain_ref[...].astype(F32)]
    parts += [qkv_ref[0, m].astype(F32) for m in range(3)]
    small = jnp.concatenate(parts, axis=0).astype(BF)
    prior = jnp.concatenate([jnp.zeros((1, 128), F32), prior_ref[0].astype(F32)], axis=0)
    tail_ref[0] = prior.astype(BF)
    for i in range(small_ref.shape[0]):
        small_ref[i] = small


def spread_kernel(small_ref, taps_ref, out_ref):
    for i in range(out_ref.shape[0]):
        out_ref[i, 0:128] = taps_ref[0]
        for x in range(4):
            out_ref[i, 128 + 16 * x : 144 + 16 * x] = small_ref[x]


def product_of(key, value, edge, small):
    key = featurize(key.astype(F32), edge[0:2], small[3:6])
    value = featurize(value.astype(F32), edge[2:4], small[6:9])
    return (key * value).astype(BF)


def product_kernel(blocks, flags_ref, key_ref, value_ref, edge_ref, small_ref, out_ref):
    first = flags_ref[0] == 0
    groups = STEP // 128
    for s in range(out_ref.shape[1] // STEP):
        cols = pl.ds(blocks[0] * 1024 + s * STEP, STEP)
        small = small_at(small_ref, blocks[0] * 8 + s * groups, groups)
        edge = edges_of(first, small, edge_ref[:, cols].astype(F32))
        product = product_of(key_ref[:, cols], value_ref[:, cols], edge[2:6], small)
        out_ref[:, pl.ds(s * STEP, STEP)] = product


def choose_taps(flags_ref, blocks, taps_refs, taps_ref):
    index, x = flags_ref[0], flags_ref[1]
    edge = jnp.where(index & 7 == 0, 1, 0)
    for place, block in enumerate(blocks):
        which = (block - x) & 3
        which = jnp.where(which == 3, 3 + edge, which)
        for step, ref in enumerate(taps_refs):

            @pl.when(which == step)
            def _():
                taps_ref[place * 8 : place * 8 + 8] = ref[:, 0:128]


def spectrum_of(before, own, forward_ref):
    signal = jnp.concatenate([before, own], axis=0)
    spectrum = dot(forward_ref[...], signal)
    return spectrum[:256] + spectrum[256:]


def spectrum_kernel(own_ref, halo_ref, forward_ref, out_ref):
    for s in range(out_ref.shape[1] // STEP):
        here = pl.ds(s * STEP, STEP)
        out_ref[:, here] = spectrum_of(halo_ref[:, here], own_ref[:, here], forward_ref)


def filter_kernel(blocks, flags_ref, query_ref, edge_ref, small_ref, own_ref, spec_ref, *refs):
    prior_refs, refs = refs[: len(blocks)], refs[len(blocks) :]
    taps_refs, (forward_ref, inverse_ref, out_ref, taps_ref, both_ref) = refs[:5], refs[5:]
    first = flags_ref[0] == 0

    @pl.when(first)
    def _():
        for s in range(out_ref.shape[1] // STEP):
            here = pl.ds(s * STEP, STEP)
            prior = []
            for i in range(STEP // 128):
                place, z = divmod(s * STEP // 128 + i, 8)
                prior.append(prior_refs[place][z])
            prior = jnp.concatenate(prior, axis=1)
            both_ref[:, here] = spectrum_of(prior, own_ref[:, here], forward_ref)

    @pl.when(jnp.logical_not(first))
    def _():
        both_ref[...] = spec_ref[...]

    choose_taps(flags_ref, blocks, taps_refs, taps_ref)
    groups = STEP // 128
    for s in range(out_ref.shape[1] // STEP):
        here = pl.ds(s * STEP, STEP)
        cols = pl.ds(blocks[0] * 1024 + s * STEP, STEP)
        small = small_at(small_ref, blocks[0] * 8 + s * groups, groups)
        edge = edges_of(first, small, edge_ref[:, cols].astype(F32))
        query = featurize(query_ref[:, cols].astype(F32), edge[0:2], small[0:3])
        taps = taps_ref[pl.ds(s * groups, groups)].reshape(STEP, 128)
        spec_h = dot_nt(forward_ref[:, 0:128], taps)
        spec_h = spec_h[:256] + spec_h[256:]
        xc, xs = both_ref[0:128, here], both_ref[128:256, here]
        hc, hs = spec_h[:128], spec_h[128:]
        spec_y = jnp.concatenate([xc * hc - xs * hs, xc * hs + xs * hc], axis=0)
        y_hi = spec_y.astype(BF)
        y_lo = (spec_y - y_hi.astype(F32)).astype(BF)
        both = dot(inverse_ref[...], y_hi)
        filtered = both[:128] + both[128:] + dot(inverse_ref[0:128, :], y_lo)
        own = own_ref[:, here].astype(F32)
        out_ref[:, here] = (query * (filtered + small[9:10] * own)).astype(BF)


def shift_by_one(value, axes, count):
    return lax.ppermute(value, axes, [(i, (i + 1) % count) for i in range(count)])


def exchange(copies, axis):
    return lax.all_to_all(copies, axis, split_axis=0, concat_axis=0, tiled=True)


def whole(shape):
    return pl.BlockSpec(shape, lambda *_: (0,) * len(shape))


def body(
    query_rows, key_rows, value_rows, short_taps, long_taps, skip_gain, prior_qkv, prior_product
):
    n_x, n_z = lax.axis_size("ctx_x"), lax.axis_size("ctx_z")
    n_ctx = n_x * n_z
    n_section = lax.axis_size("section")
    rows, channels = query_rows.shape
    ctx = ("ctx_x", "ctx_z")
    flags = jnp.stack([lax.axis_index(ctx), lax.axis_index("ctx_x")]).astype(jnp.int32)
    params = pltpu.CompilerParams(vmem_limit_bytes=24 * 1024 * 1024)
    smem = pl.BlockSpec(memory_space=pltpu.SMEM)
    vmem = pl.BlockSpec(memory_space=pltpu.VMEM)

    def in_hbm(value):
        return pltpu.with_memory_space_constraint(value, pltpu.HBM)

    last_rows = pl.BlockSpec((8, channels), lambda j: (rows // 8 - 1, 0))
    prepared = [(8, channels), (n_x, 16, 128), (1, 128, 128)]
    edge_own, small_own, tail = pl.pallas_call(
        prepare_kernel,
        grid=(1,),
        in_specs=[
            last_rows,
            last_rows,
            last_rows,
            whole(short_taps.shape),
            whole(skip_gain.shape),
            whole(prior_qkv.shape),
            whole(prior_product.shape),
        ],
        out_specs=[whole(shape) for shape in prepared],
        out_shape=[jax.ShapeDtypeStruct(shape, BF) for shape in prepared],
        compiler_params=params,
        name="prepare",
    )(
        *map(in_hbm, (query_rows, key_rows, value_rows)),
        *map(in_hbm, (short_taps, skip_gain, prior_qkv, prior_product)),
    )

    def send(value, pairs):
        return lax.ppermute(value, ctx, pairs)

    def shift(value, steps):
        return send(value, [(i, (i + steps) % n_ctx) for i in range(n_ctx)])

    def shift_x(value, steps):
        return lax.ppermute(value, "ctx_x", [(i, (i + steps) % n_x) for i in range(n_x)])

    def send_z(value, step, stops):
        return send(value, [(x * n_z + z + step, x * n_z + z) for x in range(n_x) for z in stops])

    edge = shift(edge_own, 1)
    along_x = exchange(small_own, "ctx_x")
    tails = [tail] + [send_z(tail, step, (0, 4)) for step in (1, 2, 3)]
    tail = jnp.concatenate(tails, axis=0)
    along_x, tail = lax.optimization_barrier((along_x, tail))
    spread = pl.pallas_call(
        spread_kernel,
        in_specs=[vmem, vmem],
        out_specs=vmem,
        out_shape=jax.ShapeDtypeStruct((n_z, 192, 128), BF),
        compiler_params=params,
        name="spread",
    )(along_x, long_taps)
    along_z = exchange(spread, "ctx_z")
    last_tail = send_z(tail, 4, (0,))
    along_z, edge, tail, last_tail = lax.optimization_barrier((along_z, edge, tail, last_tail))
    tail = jnp.concatenate([tail, last_tail], axis=0)

    products, halos = [], []
    for blocks in BLOCKS:
        product = pl.pallas_call(
            functools.partial(product_kernel, blocks),
            in_specs=[smem] + [vmem] * 4,
            out_specs=vmem,
            out_shape=jax.ShapeDtypeStruct((rows, 1024 * len(blocks)), BF),
            compiler_params=params,
            name="gated_product",
        )(flags, key_rows, value_rows, edge, along_z)
        products.append(product)
        halos.append(shift(product, 1))

    taps, tail, *products = lax.optimization_barrier((along_z, tail, *products))
    taps = taps[:, 0:128]
    inner = [(x * n_z + z, (x + 1) % n_x * n_z + z) for x in range(n_x) for z in range(1, n_z)]
    taps_before = send(taps, inner)
    taps_after = send(taps, [(i, (i - n_z) % n_ctx) for i in range(n_ctx)])
    prior_one = send(tail, [(n_z, 0), (2 * n_z, n_z)])
    prior_three = send(tail, [(3 * n_z, 0)])
    taps_after, taps_before, prior_one = lax.optimization_barrier(
        (taps_after, taps_before, prior_one)
    )
    taps_two = send(taps_after, [(i, (i - n_z) % n_ctx) for i in range(n_ctx)])
    taps_first = send(taps_before, [(x * n_z + 1, x * n_z) for x in range(n_x)])
    prior_two = send(prior_one, [(n_z, 0)])
    all_taps = [taps, taps_after, taps_two, taps_before, taps_first]
    priors = [tail, prior_one, prior_two, prior_three]

    forward, inverse = dft_matrices()
    handed = []
    for number, blocks in enumerate(BLOCKS):
        width = 1024 * len(blocks)
        spectrum = pl.pallas_call(
            spectrum_kernel,
            in_specs=[vmem] * 3,
            out_specs=vmem,
            out_shape=jax.ShapeDtypeStruct((256, width), F32),
            compiler_params=params,
            cost_estimate=pl.CostEstimate(
                flops=HINT, bytes_accessed=2 * 256 * width, transcendentals=0
            ),
            name="product_spectrum",
        )(products[number], halos[number], forward)
        mixed = pl.pallas_call(
            functools.partial(filter_kernel, blocks),
            in_specs=[smem] + [vmem] * (12 + len(blocks)),
            out_specs=vmem,
            out_shape=jax.ShapeDtypeStruct((rows, width), BF),
            scratch_shapes=[
                pltpu.VMEM((8 * len(blocks), 128, 128), BF),
                pltpu.VMEM((256, width), F32),
            ],
            compiler_params=params,
            name="filter_and_gate",
        )(
            flags, query_rows, edge, along_z, products[number], spectrum,
            *[priors[x] for x in blocks], *all_taps, forward, inverse,
        )
        handed.append(shift_by_one(mixed, "section", n_section))
    return jnp.concatenate(handed, axis=1)


def solution(mesh):
    n_ctx = mesh.shape["ctx"]
    n_z = 8
    inner = Mesh(
        mesh.devices.reshape(mesh.shape["section"], n_ctx // n_z, n_z), ("section", "ctx_x", "ctx_z")
    )
    ctx = ("ctx_x", "ctx_z")
    in_specs = (
        P(("section",) + ctx, None),
        P(("section",) + ctx, None),
        P(("section",) + ctx, None),
        P("section", None, None, ctx),
        P("section", ctx, None),
        P("section", ctx),
        P("section", None, None, ctx),
        P("section", None, ctx),
    )
    out_specs = P(("section",) + ctx, None)
    return jax.shard_map(body, mesh=inner, in_specs=in_specs, out_specs=out_specs, check_vma=False)
```

```python
import functools

import jax
import jax.numpy as jnp
import numpy as np
from jax import lax
from jax.experimental import pallas as pl
from jax.experimental.pallas import tpu as pltpu
from jax.sharding import Mesh
from jax.sharding import PartitionSpec as P

BF = jnp.bfloat16
F32 = jnp.float32
STEP = 512
BLOCKS = ((0, 1), (2, 3))
HINT = 20 * 10**9


def stacked_hi_lo(matrix):
    high = matrix.astype(np.float32).astype(BF)
    low = (matrix - high.astype(np.float64)).astype(np.float32).astype(BF)
    return np.concatenate([high, low], axis=0)


def dft_matrices():
    n = np.arange(256, dtype=np.float64)[None, :]
    k = np.arange(128, dtype=np.float64)[:, None]
    angle = np.pi * (2 * k + 1) * n / 256
    forward = np.concatenate([np.cos(angle), np.sin(angle)], axis=0)
    inverse = forward.T[128:] / 128
    return stacked_hi_lo(forward), stacked_hi_lo(inverse)


def dot(a, b):
    return lax.dot_general(a, b, (((1,), (0,)), ((), ())), preferred_element_type=F32)


def dot_nt(a, b):
    return lax.dot_general(a, b, (((1,), (1,)), ((), ())), preferred_element_type=F32)


def featurize(rows, before, weights):
    index = lax.broadcasted_iota(jnp.int32, rows.shape, 0)
    back_one = jnp.where(index == 0, before[1:2], pltpu.roll(rows, 1, 0))
    back_two = jnp.where(
        index == 0, before[0:1], jnp.where(index == 1, before[1:2], pltpu.roll(rows, 2, 0))
    )
    return weights[0:1] * rows + weights[1:2] * back_one + weights[2:3] * back_two


def edges_of(first, small, edge):
    return jnp.where(first, small[10:16], edge[0:6])


def small_at(ref, start, count):
    parts = []
    for g in range(start, start + count):
        low = 128 + 16 * (g // 8)
        parts.append(ref[g % 8, low : low + 16].astype(F32))
    return jnp.concatenate(parts, axis=1)


def lanes(ref, start, count):
    return jnp.concatenate([ref[start + i].astype(F32) for i in range(count)], axis=1)


def prepare_kernel(
    query_ref, key_ref, value_ref, short_ref, gain_ref, qkv_ref, prior_ref,
    edge_ref, small_ref, tail_ref,
):
    ends = [ref[...].astype(F32)[6:8] for ref in (query_ref, key_ref, value_ref)]
    edge_ref[...] = jnp.concatenate(ends + ends[2:], axis=0).astype(BF)
    parts = [short_ref[0, m].astype(F32) for m in range(3)] + [gain_ref[...].astype(F32)]
    parts += [qkv_ref[0, m].astype(F32) for m in range(3)]
    small = jnp.concatenate(parts, axis=0).astype(BF)
    prior = jnp.concatenate([jnp.zeros((1, 128), F32), prior_ref[0].astype(F32)], axis=0)
    tail_ref[0] = prior.astype(BF)
    for i in range(small_ref.shape[0]):
        small_ref[i] = small


def spread_kernel(small_ref, taps_ref, tail_ref, out_ref):
    for i in range(out_ref.shape[0]):
        out_ref[i, 0:128] = taps_ref[0]
        for x in range(4):
            out_ref[i, 128 + 16 * x : 144 + 16 * x] = small_ref[x]
        out_ref[i, 192:320] = tail_ref[0]


def product_of(key, value, edge, small):
    key = featurize(key.astype(F32), edge[0:2], small[3:6])
    value = featurize(value.astype(F32), edge[2:4], small[6:9])
    return (key * value).astype(BF)


def product_kernel(blocks, flags_ref, key_ref, value_ref, edge_ref, small_ref, out_ref):
    first = flags_ref[0] == 0
    groups = STEP // 128
    for s in range(out_ref.shape[1] // STEP):
        cols = pl.ds(blocks[0] * 1024 + s * STEP, STEP)
        small = small_at(small_ref, blocks[0] * 8 + s * groups, groups)
        edge = edges_of(first, small, edge_ref[:, cols].astype(F32))
        product = product_of(key_ref[:, cols], value_ref[:, cols], edge[2:6], small)
        out_ref[:, pl.ds(s * STEP, STEP)] = product


def choose_taps(flags_ref, blocks, taps_refs, taps_ref):
    index, x = flags_ref[0], flags_ref[1]
    more = jnp.where(index & 7 == 0, 1, 0)
    for place, block in enumerate(blocks):
        which = (block - x) & 3
        which = jnp.where(which == 3, which + more, which)
        for step, ref in enumerate(taps_refs):

            @pl.when(which == step)
            def _():
                taps_ref[place * 8 : place * 8 + 8] = ref[:, 0:128]


def spectrum_of(before, own, forward_ref):
    signal = jnp.concatenate([before, own], axis=0)
    spectrum = dot(forward_ref[...], signal)
    return spectrum[:256] + spectrum[256:]


def spectrum_kernel(own_ref, halo_ref, forward_ref, out_ref):
    for s in range(out_ref.shape[1] // STEP):
        here = pl.ds(s * STEP, STEP)
        out_ref[:, here] = spectrum_of(halo_ref[:, here], own_ref[:, here], forward_ref)


def filter_kernel(blocks, flags_ref, query_ref, edge_ref, small_ref, own_ref, spec_ref, *refs):
    prior_refs, refs = refs[: len(blocks)], refs[len(blocks) :]
    taps_refs, (forward_ref, inverse_ref, out_ref, taps_ref, both_ref) = refs[:5], refs[5:]
    first = flags_ref[0] == 0

    @pl.when(first)
    def _():
        for s in range(out_ref.shape[1] // STEP):
            here = pl.ds(s * STEP, STEP)
            prior = []
            for i in range(STEP // 128):
                place, z = divmod(s * STEP // 128 + i, 8)
                prior.append(prior_refs[place][z])
            prior = jnp.concatenate(prior, axis=1)
            both_ref[:, here] = spectrum_of(prior, own_ref[:, here], forward_ref)

    @pl.when(jnp.logical_not(first))
    def _():
        both_ref[...] = spec_ref[...]

    choose_taps(flags_ref, blocks, taps_refs, taps_ref)
    groups = STEP // 128
    for s in range(out_ref.shape[1] // STEP):
        here = pl.ds(s * STEP, STEP)
        cols = pl.ds(blocks[0] * 1024 + s * STEP, STEP)
        small = small_at(small_ref, blocks[0] * 8 + s * groups, groups)
        edge = edges_of(first, small, edge_ref[:, cols].astype(F32))
        query = featurize(query_ref[:, cols].astype(F32), edge[0:2], small[0:3])
        taps = taps_ref[pl.ds(s * groups, groups)].reshape(STEP, 128)
        spec_h = dot_nt(forward_ref[:, 0:128], taps)
        spec_h = spec_h[:256] + spec_h[256:]
        xc, xs = both_ref[0:128, here], both_ref[128:256, here]
        hc, hs = spec_h[:128], spec_h[128:]
        spec_y = jnp.concatenate([xc * hc - xs * hs, xc * hs + xs * hc], axis=0)
        y_hi = spec_y.astype(BF)
        y_lo = (spec_y - y_hi.astype(F32)).astype(BF)
        both = dot(inverse_ref[...], y_hi)
        filtered = both[:128] + both[128:] + dot(inverse_ref[0:128, :], y_lo)
        own = own_ref[:, here].astype(F32)
        out_ref[:, here] = (query * (filtered + small[9:10] * own)).astype(BF)


def shift_by_one(value, axes, count):
    return lax.ppermute(value, axes, [(i, (i + 1) % count) for i in range(count)])


def exchange(copies, axis):
    return lax.all_to_all(copies, axis, split_axis=0, concat_axis=0, tiled=True)


def whole(shape):
    return pl.BlockSpec(shape, lambda *_: (0,) * len(shape))


def body(
    query_rows, key_rows, value_rows, short_taps, long_taps, skip_gain, prior_qkv, prior_product
):
    n_x, n_z = lax.axis_size("ctx_x"), lax.axis_size("ctx_z")
    n_ctx = n_x * n_z
    n_section = lax.axis_size("section")
    rows, channels = query_rows.shape
    ctx = ("ctx_x", "ctx_z")
    flags = jnp.stack([lax.axis_index(ctx), lax.axis_index("ctx_x")]).astype(jnp.int32)
    params = pltpu.CompilerParams(vmem_limit_bytes=24 * 1024 * 1024)
    smem = pl.BlockSpec(memory_space=pltpu.SMEM)
    vmem = pl.BlockSpec(memory_space=pltpu.VMEM)

    def in_hbm(value):
        return pltpu.with_memory_space_constraint(value, pltpu.HBM)

    last_rows = pl.BlockSpec((8, channels), lambda j: (rows // 8 - 1, 0))
    prepared = [(8, channels), (n_x, 16, 128), (1, 128, 128)]
    edge_own, small_own, tail = pl.pallas_call(
        prepare_kernel,
        grid=(1,),
        in_specs=[
            last_rows,
            last_rows,
            last_rows,
            whole(short_taps.shape),
            whole(skip_gain.shape),
            whole(prior_qkv.shape),
            whole(prior_product.shape),
        ],
        out_specs=[whole(shape) for shape in prepared],
        out_shape=[jax.ShapeDtypeStruct(shape, BF) for shape in prepared],
        compiler_params=params,
        name="prepare",
    )(
        *map(in_hbm, (query_rows, key_rows, value_rows)),
        *map(in_hbm, (short_taps, skip_gain, prior_qkv, prior_product)),
    )

    def send(value, pairs):
        return lax.ppermute(value, ctx, pairs)

    def shift(value, steps):
        return send(value, [(i, (i + steps) % n_ctx) for i in range(n_ctx)])

    def shift_x(value, steps):
        return lax.ppermute(value, "ctx_x", [(i, (i + steps) % n_x) for i in range(n_x)])

    edge = shift(edge_own, 1)
    along_x = exchange(small_own, "ctx_x")
    spread = pl.pallas_call(
        spread_kernel,
        in_specs=[vmem] * 3,
        out_specs=vmem,
        out_shape=jax.ShapeDtypeStruct((n_z, 320, 128), BF),
        compiler_params=params,
        name="spread",
    )(along_x, long_taps, tail)
    along_z = exchange(spread, "ctx_z")
    along_z, edge = lax.optimization_barrier((along_z, edge))

    products, halos = [], []
    for blocks in BLOCKS:
        product = pl.pallas_call(
            functools.partial(product_kernel, blocks),
            in_specs=[smem] + [vmem] * 4,
            out_specs=vmem,
            out_shape=jax.ShapeDtypeStruct((rows, 1024 * len(blocks)), BF),
            compiler_params=params,
            name="gated_product",
        )(flags, key_rows, value_rows, edge, along_z)
        products.append(product)
        halos.append(shift(product, 1))

    wide, *products = lax.optimization_barrier((along_z, *products))
    taps = wide[:, 0:128]
    tail = wide[:, 192:320]

    def send_x(value, steps, first_z):
        pairs = [
            (x * n_z + z, (x + steps) % n_x * n_z + z) for x in range(n_x) for z in range(first_z, n_z)
        ]
        return send(value, pairs)

    def down(value):
        return send(value, [(x * n_z + 1, x * n_z) for x in range(n_x)])

    taps_after = send_x(taps, -1, 0)
    taps_before = send_x(taps, 1, 1)
    prior_one = send(tail, [(n_z, 0), (2 * n_z, n_z)])
    prior_three = send(tail, [(3 * n_z, 0)])
    taps_after, taps_before, prior_one = lax.optimization_barrier(
        (taps_after, taps_before, prior_one)
    )
    all_taps = [taps, taps_after, send_x(taps_after, -1, 0), taps_before, down(taps_before)]
    priors = [tail, prior_one, send(prior_one, [(n_z, 0)]), prior_three]

    forward, inverse = dft_matrices()
    handed = []
    for number, blocks in enumerate(BLOCKS):
        width = 1024 * len(blocks)
        spectrum = pl.pallas_call(
            spectrum_kernel,
            in_specs=[vmem] * 3,
            out_specs=vmem,
            out_shape=jax.ShapeDtypeStruct((256, width), F32),
            compiler_params=params,
            cost_estimate=pl.CostEstimate(
                flops=HINT, bytes_accessed=2 * 256 * width, transcendentals=0
            ),
            name="product_spectrum",
        )(products[number], halos[number], forward)
        mixed = pl.pallas_call(
            functools.partial(filter_kernel, blocks),
            in_specs=[smem] + [vmem] * (12 + len(blocks)),
            out_specs=vmem,
            out_shape=jax.ShapeDtypeStruct((rows, width), BF),
            scratch_shapes=[
                pltpu.VMEM((8 * len(blocks), 128, 128), BF),
                pltpu.VMEM((256, width), F32),
            ],
            compiler_params=params,
            name="filter_and_gate",
        )(
            flags, query_rows, edge, along_z, products[number], spectrum,
            *[priors[x] for x in blocks], *all_taps, forward, inverse,
        )
        handed.append(shift_by_one(mixed, "section", n_section))
    return jnp.concatenate(handed, axis=1)


def solution(mesh):
    n_ctx = mesh.shape["ctx"]
    n_z = 8
    inner = Mesh(
        mesh.devices.reshape(mesh.shape["section"], n_ctx // n_z, n_z), ("section", "ctx_x", "ctx_z")
    )
    ctx = ("ctx_x", "ctx_z")
    in_specs = (
        P(("section",) + ctx, None),
        P(("section",) + ctx, None),
        P(("section",) + ctx, None),
        P("section", None, None, ctx),
        P("section", ctx, None),
        P("section", ctx),
        P("section", None, None, ctx),
        P("section", None, ctx),
    )
    out_specs = P(("section",) + ctx, None)
    return jax.shard_map(body, mesh=inner, in_specs=in_specs, out_specs=out_specs, check_vma=False)
```

```python
import functools

import jax
import jax.numpy as jnp
import numpy as np
from jax import lax
from jax.experimental import pallas as pl
from jax.experimental.pallas import tpu as pltpu
from jax.sharding import Mesh
from jax.sharding import PartitionSpec as P

BF = jnp.bfloat16
F32 = jnp.float32
STEP = 512
BLOCKS = ((0, 1), (2, 3))
HINT = 20 * 10**9


def stacked_hi_lo(matrix):
    high = matrix.astype(np.float32).astype(BF)
    low = (matrix - high.astype(np.float64)).astype(np.float32).astype(BF)
    return np.concatenate([high, low], axis=0)


def dft_matrices():
    n = np.arange(256, dtype=np.float64)[None, :]
    k = np.arange(128, dtype=np.float64)[:, None]
    angle = np.pi * (2 * k + 1) * n / 256
    forward = np.concatenate([np.cos(angle), np.sin(angle)], axis=0)
    inverse = forward.T[128:] / 128
    return stacked_hi_lo(forward), stacked_hi_lo(inverse)


def dot(a, b):
    return lax.dot_general(a, b, (((1,), (0,)), ((), ())), preferred_element_type=F32)


def dot_nt(a, b):
    return lax.dot_general(a, b, (((1,), (1,)), ((), ())), preferred_element_type=F32)


def featurize(rows, before, weights):
    index = lax.broadcasted_iota(jnp.int32, rows.shape, 0)
    back_one = jnp.where(index == 0, before[1:2], pltpu.roll(rows, 1, 0))
    back_two = jnp.where(
        index == 0, before[0:1], jnp.where(index == 1, before[1:2], pltpu.roll(rows, 2, 0))
    )
    return weights[0:1] * rows + weights[1:2] * back_one + weights[2:3] * back_two


def edges_of(first, small, edge):
    return jnp.where(first, small[10:16], edge[0:6])


def small_at(ref, start, count):
    parts = []
    for g in range(start, start + count):
        low = 128 + 16 * (g // 8)
        parts.append(ref[g % 8, low : low + 16].astype(F32))
    return jnp.concatenate(parts, axis=1)


def lanes(ref, start, count):
    return jnp.concatenate([ref[start + i].astype(F32) for i in range(count)], axis=1)


def prepare_kernel(
    query_ref, key_ref, value_ref, short_ref, gain_ref, qkv_ref, prior_ref,
    edge_ref, small_ref, tail_ref,
):
    ends = [ref[...].astype(F32)[6:8] for ref in (query_ref, key_ref, value_ref)]
    edge_ref[...] = jnp.concatenate(ends + ends[2:], axis=0).astype(BF)
    parts = [short_ref[0, m].astype(F32) for m in range(3)] + [gain_ref[...].astype(F32)]
    parts += [qkv_ref[0, m].astype(F32) for m in range(3)]
    small = jnp.concatenate(parts, axis=0).astype(BF)
    prior = jnp.concatenate([jnp.zeros((1, 128), F32), prior_ref[0].astype(F32)], axis=0)
    tail_ref[0] = prior.astype(BF)
    for i in range(small_ref.shape[0]):
        small_ref[i] = small


def spread_kernel(small_ref, taps_ref, tail_ref, out_ref):
    for i in range(out_ref.shape[0]):
        out_ref[i, 0:128] = taps_ref[0]
        for x in range(4):
            out_ref[i, 128 + 16 * x : 144 + 16 * x] = small_ref[x]
        out_ref[i, 192:320] = tail_ref[0]


def product_of(key, value, edge, small):
    key = featurize(key.astype(F32), edge[0:2], small[3:6])
    value = featurize(value.astype(F32), edge[2:4], small[6:9])
    return (key * value).astype(BF)


def product_kernel(blocks, flags_ref, key_ref, value_ref, edge_ref, small_ref, out_ref):
    first = flags_ref[0] == 0
    groups = STEP // 128
    for s in range(out_ref.shape[1] // STEP):
        cols = pl.ds(blocks[0] * 1024 + s * STEP, STEP)
        small = small_at(small_ref, blocks[0] * 8 + s * groups, groups)
        edge = edges_of(first, small, edge_ref[:, cols].astype(F32))
        product = product_of(key_ref[:, cols], value_ref[:, cols], edge[2:6], small)
        out_ref[:, pl.ds(s * STEP, STEP)] = product


def choose_taps(flags_ref, blocks, taps_refs, taps_ref):
    index, x = flags_ref[0], flags_ref[1]
    more = jnp.where(index & 7 == 0, 1, 0)
    for place, block in enumerate(blocks):
        which = (block - x) & 3
        which = jnp.where(which == 3, which + more, which)
        for step, ref in enumerate(taps_refs):

            @pl.when(which == step)
            def _():
                taps_ref[place * 8 : place * 8 + 8] = ref[:, 0:128]


def spectrum_of(before, own, forward_ref):
    signal = jnp.concatenate([before, own], axis=0)
    spectrum = dot(forward_ref[...], signal)
    return spectrum[:256] + spectrum[256:]


def spectrum_kernel(own_ref, halo_ref, forward_ref, out_ref):
    for s in range(out_ref.shape[1] // STEP):
        here = pl.ds(s * STEP, STEP)
        out_ref[:, here] = spectrum_of(halo_ref[:, here], own_ref[:, here], forward_ref)


def filter_kernel(blocks, offset, flags_ref, query_ref, edge_ref, small_ref, own_ref, spec_ref, *refs):
    prior_refs, refs = refs[: len(blocks)], refs[len(blocks) :]
    taps_refs, (forward_ref, inverse_ref, out_ref, taps_ref, both_ref) = refs[:5], refs[5:]
    first = flags_ref[0] == 0

    @pl.when(first)
    def _():
        for s in range(out_ref.shape[1] // STEP):
            here = pl.ds(s * STEP, STEP)
            prior = []
            for i in range(STEP // 128):
                place, z = divmod(s * STEP // 128 + i, 8)
                prior.append(prior_refs[place][z])
            prior = jnp.concatenate(prior, axis=1)
            both_ref[:, here] = spectrum_of(
                prior, own_ref[:, pl.ds(offset + s * STEP, STEP)], forward_ref
            )

    @pl.when(jnp.logical_not(first))
    def _():
        both_ref[...] = spec_ref[:, pl.ds(offset, out_ref.shape[1])]

    choose_taps(flags_ref, blocks, taps_refs, taps_ref)
    groups = STEP // 128
    for s in range(out_ref.shape[1] // STEP):
        here = pl.ds(s * STEP, STEP)
        cols = pl.ds(blocks[0] * 1024 + s * STEP, STEP)
        small = small_at(small_ref, blocks[0] * 8 + s * groups, groups)
        edge = edges_of(first, small, edge_ref[:, cols].astype(F32))
        query = featurize(query_ref[:, cols].astype(F32), edge[0:2], small[0:3])
        taps = taps_ref[pl.ds(s * groups, groups)].reshape(STEP, 128)
        spec_h = dot_nt(forward_ref[:, 0:128], taps)
        spec_h = spec_h[:256] + spec_h[256:]
        xc, xs = both_ref[0:128, here], both_ref[128:256, here]
        hc, hs = spec_h[:128], spec_h[128:]
        spec_y = jnp.concatenate([xc * hc - xs * hs, xc * hs + xs * hc], axis=0)
        y_hi = spec_y.astype(BF)
        y_lo = (spec_y - y_hi.astype(F32)).astype(BF)
        both = dot(inverse_ref[...], y_hi)
        filtered = both[:128] + both[128:] + dot(inverse_ref[0:128, :], y_lo)
        own = own_ref[:, pl.ds(offset + s * STEP, STEP)].astype(F32)
        out_ref[:, here] = (query * (filtered + small[9:10] * own)).astype(BF)


def shift_by_one(value, axes, count):
    return lax.ppermute(value, axes, [(i, (i + 1) % count) for i in range(count)])


def exchange(copies, axis):
    return lax.all_to_all(copies, axis, split_axis=0, concat_axis=0, tiled=True)


def whole(shape):
    return pl.BlockSpec(shape, lambda *_: (0,) * len(shape))


def body(
    query_rows, key_rows, value_rows, short_taps, long_taps, skip_gain, prior_qkv, prior_product
):
    n_x, n_z = lax.axis_size("ctx_x"), lax.axis_size("ctx_z")
    n_ctx = n_x * n_z
    n_section = lax.axis_size("section")
    rows, channels = query_rows.shape
    ctx = ("ctx_x", "ctx_z")
    flags = jnp.stack([lax.axis_index(ctx), lax.axis_index("ctx_x")]).astype(jnp.int32)
    params = pltpu.CompilerParams(vmem_limit_bytes=24 * 1024 * 1024)
    smem = pl.BlockSpec(memory_space=pltpu.SMEM)
    vmem = pl.BlockSpec(memory_space=pltpu.VMEM)

    def in_hbm(value):
        return pltpu.with_memory_space_constraint(value, pltpu.HBM)

    last_rows = pl.BlockSpec((8, channels), lambda j: (rows // 8 - 1, 0))
    prepared = [(8, channels), (n_x, 16, 128), (1, 128, 128)]
    edge_own, small_own, tail = pl.pallas_call(
        prepare_kernel,
        grid=(1,),
        in_specs=[
            last_rows,
            last_rows,
            last_rows,
            whole(short_taps.shape),
            whole(skip_gain.shape),
            whole(prior_qkv.shape),
            whole(prior_product.shape),
        ],
        out_specs=[whole(shape) for shape in prepared],
        out_shape=[jax.ShapeDtypeStruct(shape, BF) for shape in prepared],
        compiler_params=params,
        name="prepare",
    )(
        *map(in_hbm, (query_rows, key_rows, value_rows)),
        *map(in_hbm, (short_taps, skip_gain, prior_qkv, prior_product)),
    )

    def send(value, pairs):
        return lax.ppermute(value, ctx, pairs)

    def shift(value, steps):
        return send(value, [(i, (i + steps) % n_ctx) for i in range(n_ctx)])

    def shift_x(value, steps):
        return lax.ppermute(value, "ctx_x", [(i, (i + steps) % n_x) for i in range(n_x)])

    edge = shift(edge_own, 1)
    along_x = exchange(small_own, "ctx_x")
    spread = pl.pallas_call(
        spread_kernel,
        in_specs=[vmem] * 3,
        out_specs=vmem,
        out_shape=jax.ShapeDtypeStruct((n_z, 320, 128), BF),
        compiler_params=params,
        name="spread",
    )(along_x, long_taps, tail)
    along_z = exchange(spread, "ctx_z")
    along_z, edge = lax.optimization_barrier((along_z, edge))

    products, halos = [], []
    for blocks in BLOCKS:
        product = pl.pallas_call(
            functools.partial(product_kernel, blocks),
            in_specs=[smem] + [vmem] * 4,
            out_specs=vmem,
            out_shape=jax.ShapeDtypeStruct((rows, 1024 * len(blocks)), BF),
            compiler_params=params,
            name="gated_product",
        )(flags, key_rows, value_rows, edge, along_z)
        products.append(product)
        halos.append(shift(product, 1))

    wide, *products = lax.optimization_barrier((along_z, *products))
    taps = wide[:, 0:128]
    tail = wide[:, 192:320]

    def send_x(value, steps, first_z):
        pairs = [
            (x * n_z + z, (x + steps) % n_x * n_z + z) for x in range(n_x) for z in range(first_z, n_z)
        ]
        return send(value, pairs)

    def down(value):
        return send(value, [(x * n_z + 1, x * n_z) for x in range(n_x)])

    taps_after = send_x(taps, -1, 0)
    taps_before = send_x(taps, 1, 1)
    prior_one = send(tail, [(n_z, 0), (2 * n_z, n_z)])
    prior_three = send(tail, [(3 * n_z, 0)])
    taps_after, taps_before, prior_one = lax.optimization_barrier(
        (taps_after, taps_before, prior_one)
    )
    all_taps = [taps, taps_after, send_x(taps_after, -1, 0), taps_before, down(taps_before)]
    priors = [tail, prior_one, send(prior_one, [(n_z, 0)]), prior_three]

    forward, inverse = dft_matrices()
    handed = []
    for number, blocks in enumerate(BLOCKS):
        width = 1024 * len(blocks)
        spectrum = pl.pallas_call(
            spectrum_kernel,
            in_specs=[vmem] * 3,
            out_specs=vmem,
            out_shape=jax.ShapeDtypeStruct((256, width), F32),
            compiler_params=params,
            cost_estimate=pl.CostEstimate(
                flops=HINT, bytes_accessed=2 * 256 * width, transcendentals=0
            ),
            name="product_spectrum",
        )(products[number], halos[number], forward)
        for part in [blocks] if number == 0 else [(x,) for x in blocks]:
            mixed = pl.pallas_call(
                functools.partial(filter_kernel, part, 1024 * (part[0] - blocks[0])),
                in_specs=[smem] + [vmem] * (12 + len(part)),
                out_specs=vmem,
                out_shape=jax.ShapeDtypeStruct((rows, 1024 * len(part)), BF),
                scratch_shapes=[
                    pltpu.VMEM((8 * len(part), 128, 128), BF),
                    pltpu.VMEM((256, 1024 * len(part)), F32),
                ],
                compiler_params=params,
                name="filter_and_gate",
            )(
                flags, query_rows, edge, along_z, products[number], spectrum,
                *[priors[x] for x in part], *all_taps, forward, inverse,
            )
            handed.append(shift_by_one(mixed, "section", n_section))
    return jnp.concatenate(handed, axis=1)


def solution(mesh):
    n_ctx = mesh.shape["ctx"]
    n_z = 8
    inner = Mesh(
        mesh.devices.reshape(mesh.shape["section"], n_ctx // n_z, n_z), ("section", "ctx_x", "ctx_z")
    )
    ctx = ("ctx_x", "ctx_z")
    in_specs = (
        P(("section",) + ctx, None),
        P(("section",) + ctx, None),
        P(("section",) + ctx, None),
        P("section", None, None, ctx),
        P("section", ctx, None),
        P("section", ctx),
        P("section", None, None, ctx),
        P("section", None, ctx),
    )
    out_specs = P(("section",) + ctx, None)
    return jax.shard_map(body, mesh=inner, in_specs=in_specs, out_specs=out_specs, check_vma=False)
```
